32 devices in a mesh: dp: 8 (over z, y), tensor: 4 (over x, core).
Axes of the slice: x: 2, y: 2, z: 4, core: 2. Of those that a mesh axis runs over, the one named last changes fastest.
Arguments:
- tokens: bfloat16 [2, 128, 12288], P(None, 'dp', 'tensor'), may hold values from -6 to 6
- up_weight: bfloat16 [12288, 49152], P('tensor', 'dp'), may hold values from -0.0546875 to 0.0546875
- up_bias: bfloat16 [49152], P('dp'), may hold values from -3 to 3
- down_weight: bfloat16 [49152, 12288], P('dp', 'tensor'), may hold values from -0.02734375 to 0.02734375
- down_bias: bfloat16 [12288], P('tensor'), may hold values from -3 to 3
- active: int32 [2, 1, 384], P(None, None, 'dp'), may hold values from 0 to 1
Outputs:
- mixed: bfloat16 [2, 128, 12288], P(None, 'dp', 'tensor')
The draws below stay inside these ranges and needn't reach their ends.
All inputs are finite; a program needn't handle non-finite values.
Results may differ from the reference program's by a relative error of at most 0.0042.
Values may be sent and summed in bfloat16 or wider, within the bound.
A program may use at most 128 MiB of HBM per device.

```python
import jax
import jax.numpy as jnp

D = 12288
FF = 49152
HBLK = 128
RBLK = 128
STEPS = 2
ROWS = 128


def draw_active(key, part):
    groups = FF // HBLK // 4
    levels = jax.random.randint(jax.random.fold_in(key, 11), (groups,), 1, 8)
    coins = jax.random.randint(jax.random.fold_in(key, 12), (STEPS, ROWS // RBLK, FF // HBLK), 0, 8)
    return (coins < jnp.repeat(levels, 4)[None, None, :]).astype(jnp.int32)


def shard_levels(rng, extent, pieces, low, high):
    loudness = 1.0
    for position, parts in pieces:
        heights = jax.random.uniform(jax.random.fold_in(jax.random.fold_in(rng, 6), position), (parts,), jnp.float32, low / len(pieces), high / len(pieces))
        loudness = loudness * jnp.repeat(jnp.exp(heights), extent[position] // parts).reshape((-1,) + (1,) * (len(extent) - 1 - position))
    return loudness


def gaussian(key, dims, spread, reach, cuts=(), held_as=jnp.bfloat16):
    result = jax.random.normal(key, dims, jnp.float32) * spread
    if len(cuts) > 0:
        result = shard_levels(key, dims, cuts, -0.22, 0.18) * result
    return jnp.clip(result, min=-reach, max=reach).astype(held_as)


def setup_inputs(seed: int = 0) -> dict:
    splits = jax.random.split(jax.random.key(seed), 7)
    tokens = gaussian(splits[0], (STEPS, ROWS, D), 1.0, 6.0, ((1, 8), (2, 4)))
    up_weight = gaussian(splits[1], (D, FF), D ** -0.5, 0.0546875, ((0, 4), (1, 8)))
    up_bias = gaussian(splits[2], (FF,), 0.5, 3.0, ((0, 8),))
    down_weight = gaussian(splits[3], (FF, D), FF ** -0.5, 0.02734375, ((0, 8), (1, 4)))
    down_bias = gaussian(splits[4], (D,), 0.5, 3.0, ((0, 4),))
    active = draw_active(jax.random.fold_in(splits[6], 71), 0)
    return {"tokens": tokens, "up_weight": up_weight, "up_bias": up_bias, "down_weight": down_weight, "down_bias": down_bias, "active": active}


def reference(tokens, up_weight, up_bias, down_weight, down_bias, active):
    results = []
    for step_index in range(STEPS):
        preact = jnp.dot(tokens[step_index], up_weight, preferred_element_type=jnp.float32) + up_bias.astype(jnp.float32)
        row_mask = jnp.repeat(jnp.repeat(active[step_index].astype(jnp.float32), RBLK, axis=0), HBLK, axis=1)
        hidden = (jnp.maximum(preact, 0.0) * row_mask).astype(jnp.bfloat16)
        summed = jnp.dot(hidden, down_weight, preferred_element_type=jnp.float32) + down_bias.astype(jnp.float32)
        results.append(summed.astype(jnp.bfloat16))
    return jnp.stack(results)
```

```python
import functools

import jax
import jax.numpy as jnp
from jax import lax
from jax.experimental import pallas as pl
from jax.experimental.pallas import tpu as pltpu
from jax.sharding import PartitionSpec as P

RBLK = 128
TILE = 512
LAG = 3
MESH = pl.DeviceIdType.MESH


def activate(summed, up_bias, mask_table, first_row):
    row_count = summed.shape[0]
    blocks = mask_table.shape[1]
    row_ids = first_row + jnp.arange(row_count, dtype=jnp.int32)
    onehot = (
        row_ids[:, None] // RBLK == jnp.arange(mask_table.shape[0], dtype=jnp.int32)[None, :]
    ).astype(jnp.float32)
    row_mask = jnp.dot(onehot, mask_table.astype(jnp.float32))
    preact = jnp.maximum(summed + up_bias.astype(jnp.float32), 0.0)
    gated_rows = preact.reshape(row_count, blocks, -1) * row_mask[:, :, None]
    return gated_rows.reshape(row_count, -1).astype(jnp.bfloat16)


def local(tokens, up_weight, up_bias, down_weight, down_bias, active):
    results = []
    for step_index in range(tokens.shape[0]):
        local_rows = tokens[step_index]
        mask_table = active[step_index]
        partial_up = jnp.dot(
            lax.all_gather(local_rows, "dp", axis=0, tiled=True),
            up_weight,
            preferred_element_type=jnp.float32,
        )
        row_share = lax.psum_scatter(partial_up, "tensor", scatter_dimension=0, tiled=True)
        first_row = lax.axis_index("tensor") * row_share.shape[0]
        hidden_share = activate(row_share, up_bias, mask_table, first_row)
        hidden = lax.all_gather(hidden_share, "tensor", axis=0, tiled=True)
        mixed_rows = lax.psum_scatter(
            jnp.dot(hidden, down_weight, preferred_element_type=jnp.float32),
            "dp",
            scatter_dimension=0,
            tiled=True,
        )
        results.append((mixed_rows + down_bias.astype(jnp.float32)).astype(jnp.bfloat16))
    return jnp.stack(results)


ORDER = (
    (0, 0, 1), (0, 0, 0), (0, 1, 0), (1, 0, 0),
    (1, 1, 0), (2, 0, 0), (2, 1, 0), (3, 0, 0),
    (3, 1, 0), (3, 0, 1), (3, 1, 1),
    (0, 1, 1), (1, 0, 1), (1, 1, 1), (2, 0, 1), (2, 1, 1),
)
SLOT = {key: i for i, key in enumerate(ORDER)}
CHUNKS = ((0, 4), (4, 8), (8, 16))
PARTS = ((0, 4), (4, 8), (8, 11), (11, 16))
PAIRS = (
    ((0, 0), (1, 0), (2, 0), (3, 0), (3, 1)),
    ((0, 1), (1, 1), (2, 1)),
)
HOPS = (((1, 0, 1), (2, 1, 2), (3, 2, 4)), ((1, 0, 1), (2, 1, 2)))


def fused_kernel(nt, tok, wu, wd, bias_u, active, out,
                 x_all, w, pbuf, crecv, xsend, xrecv, hid, acc,
                 ysend0, yrecv0, ysend1, yrecv1, zsend0, zrecv0, zsend1, zrecv1,
                 tsem, wsem, ag_send, ag_recv, c_send, c_recv, x_send, x_recv, h_send, h_recv,
                 y_send, y_recv, z_send, z_recv):
    f32, bf16 = jnp.float32, jnp.bfloat16
    steps, share, depth = tok.shape
    ysend, yrecv, zsend, zrecv = (ysend0, ysend1), (yrecv0, yrecv1), (zsend0, zsend1), (zrecv0, zrecv1)
    half = TILE // 2
    dp, t = lax.axis_index("dp"), lax.axis_index("tensor")
    z, y = dp // 2, dp % 2
    x, c = t // 2, t % 2
    y_peer = (z * 2 + 1 - y, t)
    x_peer = (dp, (1 - x) * 2 + c)
    c_peer = (dp, x * 2 + 1 - c)
    z_peer = (None, ((z + 1 - 2 * (z % 2)) * 2 + y, t), (lax.rem(z + 2, 4) * 2 + y, t), ((3 - z) * 2 + y, t))
    cols = lambda j: pl.ds(pl.multiple_of(j * TILE, TILE), TILE)
    side = lambda j, h: pl.ds(pl.multiple_of(j * TILE + h * half, half), half)
    nc = depth // TILE
    rows_of = lambda span: pl.ds(span[0] * share, (span[1] - span[0]) * share)
    slot = lambda *key: pl.ds(SLOT[key] * share, share)

    def rcopy(src, dst, ss, rs, dev):
        return pltpu.make_async_remote_copy(
            src_ref=src, dst_ref=dst, send_sem=ss, recv_sem=rs, device_id=dev, device_id_type=MESH
        )

    def up_load(j):
        return pltpu.make_async_copy(wu.at[:, cols(j)], w.at[j], wsem.at[j])

    def down_load(i):
        n, part = i // 2, i % 2
        lines = pl.ds(pl.multiple_of(part * depth, depth), depth)
        return pltpu.make_async_copy(wd.at[lines, cols(n)], w.at[i], wsem.at[i])

    mine = [pltpu.make_async_copy(tok.at[s], x_all.at[slot(0, 0, s)], tsem.at[s]) for s in range(steps)]
    for copy in mine:
        copy.start()

    @pl.loop(0, nt)
    def _(j):
        up_load(j).start()

    barrier = pltpu.get_barrier_semaphore()
    peers = [y_peer, x_peer, c_peer] + list(z_peer[1:])
    for peer in peers:
        pl.semaphore_signal(barrier, inc=1, device_id=peer, device_id_type=MESH)
    pl.semaphore_wait(barrier, len(peers))

    def gather(kind, s):
        src, dst, dev = (
            ((0, 0), (0, 1), y_peer),
            ((0, 0), (1, 0), z_peer[1]),
            ((0, 0), (2, 0), z_peer[2]),
            ((1, 0), (1, 1), y_peer),
            ((2, 0), (3, 0), z_peer[1]),
            ((2, 0), (2, 1), y_peer),
            ((3, 0), (3, 1), y_peer),
        )[kind]
        return rcopy(
            x_all.at[slot(*src, s)], x_all.at[slot(*dst, s)], ag_send.at[s, kind], ag_recv.at[s, kind], dev
        )

    def c_copy(ch, j):
        rows = rows_of(CHUNKS[ch])
        q = ch * nt + j
        return rcopy(pbuf.at[j, 1 - c, rows], crecv.at[j, rows], c_send.at[q], c_recv.at[q], c_peer)

    def x_copy(part, j):
        rows = rows_of(PARTS[part])
        q = part * nt + j
        return rcopy(xsend.at[j, rows], xrecv.at[j, rows], x_send.at[q], x_recv.at[q], x_peer)

    def h_copy(part, j, h):
        view = hid.at[rows_of(PARTS[part]), side(j, h)]
        q = part * nt + j
        return rcopy(view, view, h_send.at[q], h_recv.at[q], c_peer)

    def up(ch, j):
        rows = rows_of(CHUNKS[ch])
        total = jnp.dot(x_all[rows], w[j], preferred_element_type=f32)
        for h in range(2):
            pbuf[j, h, rows] = total[:, h * half : (h + 1) * half]
        c_copy(ch, j).start()

    def mid(part, j):
        rows = rows_of(PARTS[part])
        total = pbuf[j, c, rows] + crecv[j, rows]
        crecv[j, rows] = total
        xsend[j, rows] = total.astype(bf16)
        x_copy(part, j).start()

    def act(part, j):
        first, last = PARTS[part]
        rows = rows_of(PARTS[part])
        x_copy(part, j).wait_recv()
        bias = bias_u[side(j, c)].astype(f32).reshape(1, half)
        pre = jnp.maximum(crecv[j, rows] + xrecv[j, rows].astype(f32) + bias, 0.0)
        blocks = active.shape[2] // nt
        width = TILE // blocks
        for b in range(blocks // 2):
            lanes = pl.ds(pl.multiple_of(j * TILE + c * half + b * width, width), width)
            gates = [active[s, 0, j * blocks + c * (blocks // 2) + b].astype(f32) for s in range(steps)]
            i = first
            while i < last:
                n = i
                while n < last and ORDER[n][2] == ORDER[i][2]:
                    n += 1
                piece = pre[(i - first) * share : (n - first) * share, b * width : (b + 1) * width]
                hid[pl.ds(i * share, (n - i) * share), lanes] = (piece * gates[ORDER[i][2]]).astype(bf16)
                i = n
        h_copy(part, j, c).start()

    def hidden_ready(part, start, stop):
        @pl.loop(start, stop)
        def _(j):
            h_copy(part, j, 1 - c).wait_recv()

    slots_of = [[i for key in PAIRS[g] for i in (SLOT[key[0], 0, key[1]], SLOT[key[0], 1, key[1]])] for g in range(2)]
    lines_of = [sorted(slots, key=lambda i: i or len(ORDER)) for slots in slots_of]

    def hidden_rows(g, part):
        span = slice(part * depth, (part + 1) * depth)
        ids = lines_of[g]
        if ids[-1] != 0:
            return hid[ids[0] * share : (ids[-1] + 1) * share, span]
        return jnp.concatenate([hid[ids[0] * share : (ids[-2] + 1) * share, span], hid[:share, span]], axis=0)

    def y_copy(g, n):
        q = g * nc + n
        return rcopy(ysend[g].at[n], yrecv[g].at[n], y_send.at[q], y_recv.at[q], y_peer)

    def z_copy(g, n, hop):
        k, first, last = HOPS[g][hop]
        span = pl.ds(first, last - first)
        q = (g * nc + n) * 3 + hop
        return rcopy(zsend[g].at[n, span], zrecv[g].at[n, span], z_send.at[q], z_recv.at[q], z_peer[k])

    def share_out(g, n, total):
        for p, (k, s) in enumerate(PAIRS[g]):
            for e in range(2):
                i = lines_of[g].index(SLOT[k, e, s]) * share
                if e:
                    ysend[g][n, p] = total[i : i + share].astype(bf16)
                else:
                    acc[slot(k, 0, s), cols(n)] = total[i : i + share]
        y_copy(g, n).start()

    def down(n):
        total = jnp.zeros((len(lines_of[0]) * share, TILE), f32)
        for part in range(2):
            total += jnp.dot(hidden_rows(0, part), w[n * 2 + part], preferred_element_type=f32)
        share_out(0, n, total)

    def down_first(n):
        total = jnp.dot(hidden_rows(1, 0), w[n * 2], preferred_element_type=f32)
        for i, line in enumerate(lines_of[1]):
            acc[pl.ds(line * share, share), cols(n)] = total[i * share : (i + 1) * share]

    def down_second(n):
        total = jnp.concatenate([acc[pl.ds(line * share, share), cols(n)] for line in lines_of[1]], axis=0)
        total += jnp.dot(hidden_rows(1, 1), w[n * 2 + 1], preferred_element_type=f32)
        share_out(1, n, total)

    def rs_z(g, n):
        y_copy(g, n).wait_recv()
        for p, (k, s) in enumerate(PAIRS[g]):
            if k:
                pair = acc[slot(k, 0, s), cols(n)] + yrecv[g][n, p].astype(f32)
                zsend[g][n, p - 1] = pair.astype(bf16)
        for hop in range(len(HOPS[g])):
            z_copy(g, n, hop).start()

    def rs_finish(n):
        for g in range(2):
            for hop in range(len(HOPS[g])):
                z_copy(g, n, hop).wait_recv()
        for s in range(steps):
            total = acc[slot(0, 0, s), cols(n)] + yrecv[s][n, 0].astype(f32)
            for g in range(2):
                for p, (k, step) in enumerate(PAIRS[g]):
                    if k and step == s:
                        total += zrecv[g][n, p - 1].astype(f32)
            out[s, :, cols(n)] = total

    for copy in mine:
        copy.wait()
    for s in (0, 1):
        gather(0, s).start()
        gather(1, s).start()
    gather(1, 0).wait_recv()
    gather(3, 0).start()
    gather(2, 0).start()
    gather(2, 1).start()
    gather(0, 0).wait_recv()

    def first_chunk(j):
        up_load(j).wait()
        up(0, j)

        @pl.when(j >= LAG)
        def _():
            c_copy(0, j - LAG).wait_recv()
            mid(0, j - LAG)

    def forward_far(s):
        gather(2, s).wait_recv()
        gather(4, s).start()
        gather(5, s).start()

    def forward_last(s):
        gather(4, s).wait_recv()
        gather(6, s).start()

    cut = [0, nt // 4, nt // 2, nt * 3 // 4, nt]
    pl.loop(cut[0], cut[1])(first_chunk)
    gather(1, 1).wait_recv()
    gather(3, 1).start()
    pl.loop(cut[1], cut[2])(first_chunk)
    forward_far(0)
    pl.loop(cut[2], cut[3])(first_chunk)
    forward_far(1)
    pl.loop(cut[3], cut[4])(first_chunk)
    forward_last(0)
    gather(3, 0).wait_recv()
    gather(5, 0).wait_recv()

    @pl.loop(0, LAG)
    def _(j):
        up(1, j)
        c_copy(0, nt - LAG + j).wait_recv()
        mid(0, nt - LAG + j)

    forward_last(1)

    @pl.loop(LAG, nt)
    def _(j):
        up(1, j)
        c_copy(1, j - LAG).wait_recv()
        mid(1, j - LAG)
        act(0, j - LAG)

    gather(6, 0).wait_recv()
    for kind in (0, 3, 5, 6):
        gather(kind, 1).wait_recv()

    @pl.loop(0, LAG)
    def _(j):
        up(2, j)
        down_load(j).start()
        c_copy(1, nt - LAG + j).wait_recv()
        mid(1, nt - LAG + j)
        act(0, nt - LAG + j)

    @pl.loop(LAG, nt)
    def _(j):
        up(2, j)
        down_load(j).start()
        c_copy(2, j - LAG).wait_recv()
        mid(2, j - LAG)
        act(1, j - LAG)

    @pl.loop(nt - LAG, nt)
    def _(j):
        c_copy(2, j).wait_recv()
        mid(2, j)
        act(1, j)

    @pl.loop(0, nt)
    def _(j):
        mid(3, j)

    @pl.loop(0, nt)
    def _(j):
        act(2, j)

    for part in range(3):
        hidden_ready(part, 0, nt)

    @pl.loop(0, nc)
    def _(n):
        down_load(n * 2).wait()
        down_load(n * 2 + 1).wait()
        down(n)
        act(3, n)

        @pl.when(n >= LAG)
        def _():
            rs_z(0, n - LAG)

    hidden_ready(3, 0, nc)

    @pl.loop(0, nc)
    def _(n):
        down_first(n)
        act(3, nc + n)

        @pl.when(n >= nc - LAG + 1)
        def _():
            rs_z(0, n - 1)

    hidden_ready(3, nc, nt)

    @pl.loop(0, nc)
    def _(n):
        down_second(n)

        @pl.when(n == 0)
        def _():
            rs_z(0, nc - 1)

        @pl.when(n >= LAG)
        def _():
            rs_z(1, n - LAG)

    @pl.loop(nc - LAG, nc)
    def _(n):
        rs_z(1, n)

    @pl.loop(0, nc)
    def _(n):
        rs_finish(n)

    for s in range(steps):
        for kind in range(7):
            gather(kind, s).wait_send()

    @pl.loop(0, nc)
    def _(n):
        for g in range(2):
            y_copy(g, n).wait_send()
            for hop in range(len(HOPS[g])):
                z_copy(g, n, hop).wait_send()

    @pl.loop(0, nt)
    def _(j):
        for ch in range(len(CHUNKS)):
            c_copy(ch, j).wait_send()
        for part in range(len(PARTS)):
            x_copy(part, j).wait_send()
            h_copy(part, j, c).wait_send()


def fused(groups, tokens, up_weight, up_bias, down_weight, down_bias, active):
    steps, share, depth = tokens.shape
    hidden = up_weight.shape[1]
    nt, nc, rows = hidden // TILE, depth // TILE, steps * groups * share
    f32, bf16 = jnp.float32, jnp.bfloat16
    any_space, vmem = pl.BlockSpec(memory_space=pl.ANY), pl.BlockSpec(memory_space=pltpu.VMEM)
    smem = pl.BlockSpec(memory_space=pltpu.SMEM)
    dma = pltpu.SemaphoreType.DMA
    half = TILE // 2
    mixed = pl.pallas_call(
        functools.partial(fused_kernel, nt),
        out_shape=jax.ShapeDtypeStruct(tokens.shape, f32),
        in_specs=[any_space, any_space, any_space, vmem, smem],
        out_specs=vmem,
        scratch_shapes=[
            pltpu.VMEM((rows, depth), bf16),
            pltpu.VMEM((nt, depth, TILE), bf16),
            pltpu.VMEM((nt, 2, rows, half), f32),
            pltpu.VMEM((nt, rows, half), f32),
            pltpu.VMEM((nt, rows, half), bf16),
            pltpu.VMEM((nt, rows, half), bf16),
            pltpu.VMEM((rows, hidden), bf16),
            pltpu.VMEM((rows, depth), f32),
        ]
        + [pltpu.VMEM((nc, len(PAIRS[g]), share, TILE), bf16) for g in (0, 0, 1, 1)]
        + [pltpu.VMEM((nc, len(PAIRS[g]) - 1, share, TILE), bf16) for g in (0, 0, 1, 1)]
        + [
            dma((steps,)),
            dma((nt,)),
            dma((steps, 7)),
            dma((steps, 7)),
        ]
        + [dma((len(CHUNKS) * nt,))] * 2
        + [dma((len(PARTS) * nt,))] * 4
        + [dma((2 * nc,))] * 2
        + [dma((2 * nc * 3,))] * 2,
        compiler_params=pltpu.CompilerParams(
            collective_id=0, has_side_effects=True, vmem_limit_bytes=67043328
        ),
    )(tokens, up_weight, down_weight, up_bias, active)
    return (mixed + down_bias.astype(f32)).astype(bf16)


def solution(mesh):
    placed = (
        P(None, "dp", "tensor"),
        P("tensor", "dp"),
        P("dp"),
        P("dp", "tensor"),
        P("tensor"),
        P(None, None, "dp"),
    )
    groups, columns = mesh.shape["dp"], mesh.shape["tensor"]

    def body(*args):
        steps, share, depth = args[0].shape
        hidden, table = args[1].shape[1], args[5].shape
        if (
            (groups, columns, steps, table[1]) == (8, 4, 2, 1)
            and share % 16 == 0
            and depth % TILE == 0
            and hidden == 2 * depth
            and table[2] % (hidden // TILE * 2) == 0
            and depth // TILE > LAG
        ):
            return fused(groups, *args)
        return local(*args)

    return jax.shard_map(
        body, mesh=mesh, in_specs=placed, out_specs=P(None, "dp", "tensor"), check_vma=False
    )
```

```python
import functools

import jax
import jax.numpy as jnp
from jax import lax
from jax.experimental import pallas as pl
from jax.experimental.pallas import tpu as pltpu
from jax.sharding import PartitionSpec as P

RBLK = 128
TILE = 512
LAG = 3
MESH = pl.DeviceIdType.MESH


def activate(summed, up_bias, mask_table, first_row):
    row_count = summed.shape[0]
    blocks = mask_table.shape[1]
    row_ids = first_row + jnp.arange(row_count, dtype=jnp.int32)
    onehot = (
        row_ids[:, None] // RBLK == jnp.arange(mask_table.shape[0], dtype=jnp.int32)[None, :]
    ).astype(jnp.float32)
    row_mask = jnp.dot(onehot, mask_table.astype(jnp.float32))
    preact = jnp.maximum(summed + up_bias.astype(jnp.float32), 0.0)
    gated_rows = preact.reshape(row_count, blocks, -1) * row_mask[:, :, None]
    return gated_rows.reshape(row_count, -1).astype(jnp.bfloat16)


def local(tokens, up_weight, up_bias, down_weight, down_bias, active):
    results = []
    for step_index in range(tokens.shape[0]):
        local_rows = tokens[step_index]
        mask_table = active[step_index]
        partial_up = jnp.dot(
            lax.all_gather(local_rows, "dp", axis=0, tiled=True),
            up_weight,
            preferred_element_type=jnp.float32,
        )
        row_share = lax.psum_scatter(partial_up, "tensor", scatter_dimension=0, tiled=True)
        first_row = lax.axis_index("tensor") * row_share.shape[0]
        hidden_share = activate(row_share, up_bias, mask_table, first_row)
        hidden = lax.all_gather(hidden_share, "tensor", axis=0, tiled=True)
        mixed_rows = lax.psum_scatter(
            jnp.dot(hidden, down_weight, preferred_element_type=jnp.float32),
            "dp",
            scatter_dimension=0,
            tiled=True,
        )
        results.append((mixed_rows + down_bias.astype(jnp.float32)).astype(jnp.bfloat16))
    return jnp.stack(results)


ORDER = (
    (0, 0, 1), (0, 0, 0), (0, 1, 0), (1, 0, 0),
    (1, 1, 0), (2, 0, 0), (2, 1, 0), (3, 0, 0),
    (3, 1, 0), (3, 0, 1), (3, 1, 1),
    (0, 1, 1), (1, 0, 1), (1, 1, 1), (2, 0, 1), (2, 1, 1),
)
SLOT = {key: i for i, key in enumerate(ORDER)}
CHUNKS = ((0, 4), (4, 8), (8, 16))
PARTS = ((0, 4), (4, 8), (8, 11), (11, 16))
PAIRS = (
    ((0, 0), (1, 0), (2, 0), (3, 0), (3, 1)),
    ((0, 1), (1, 1), (2, 1)),
)
HOPS = (((1, 0, 1), (2, 1, 2), (3, 2, 4)), ((1, 0, 1), (2, 1, 2)))


def fused_kernel(nt, tok, wu, wd, bias_u, bias_d, active, out,
                 x_all, w, pbuf, crecv, xsend, xrecv, hid, acc,
                 ysend0, yrecv0, ysend1, yrecv1, zsend0, zrecv0, zsend1, zrecv1,
                 tsem, wsem, ag_send, ag_recv, c_send, c_recv, x_send, x_recv, h_send, h_recv,
                 y_send, y_recv, z_send, z_recv):
    f32, bf16 = jnp.float32, jnp.bfloat16
    steps, share, depth = tok.shape
    ysend, yrecv, zsend, zrecv = (ysend0, ysend1), (yrecv0, yrecv1), (zsend0, zsend1), (zrecv0, zrecv1)
    half = TILE // 2
    dp, t = lax.axis_index("dp"), lax.axis_index("tensor")
    z, y = dp // 2, dp % 2
    x, c = t // 2, t % 2
    y_peer = (z * 2 + 1 - y, t)
    x_peer = (dp, (1 - x) * 2 + c)
    c_peer = (dp, x * 2 + 1 - c)
    z_peer = (None, ((z + 1 - 2 * (z % 2)) * 2 + y, t), (lax.rem(z + 2, 4) * 2 + y, t), ((3 - z) * 2 + y, t))
    cols = lambda j: pl.ds(pl.multiple_of(j * TILE, TILE), TILE)
    side = lambda j, h: pl.ds(pl.multiple_of(j * TILE + h * half, half), half)
    nc = depth // TILE
    rows_of = lambda span: pl.ds(span[0] * share, (span[1] - span[0]) * share)
    slot = lambda *key: pl.ds(SLOT[key] * share, share)

    def rcopy(src, dst, ss, rs, dev):
        return pltpu.make_async_remote_copy(
            src_ref=src, dst_ref=dst, send_sem=ss, recv_sem=rs, device_id=dev, device_id_type=MESH
        )

    def up_load(j):
        return pltpu.make_async_copy(wu.at[:, cols(j)], w.at[j], wsem.at[j])

    def down_load(i):
        n, part = i // 2, i % 2
        lines = pl.ds(pl.multiple_of(part * depth, depth), depth)
        return pltpu.make_async_copy(wd.at[lines, cols(n)], w.at[i], wsem.at[i])

    mine = [pltpu.make_async_copy(tok.at[s], x_all.at[slot(0, 0, s)], tsem.at[s]) for s in range(steps)]
    for copy in mine:
        copy.start()

    @pl.loop(0, nt)
    def _(j):
        up_load(j).start()

    barrier = pltpu.get_barrier_semaphore()
    peers = [y_peer, x_peer, c_peer] + list(z_peer[1:])
    for peer in peers:
        pl.semaphore_signal(barrier, inc=1, device_id=peer, device_id_type=MESH)
    pl.semaphore_wait(barrier, len(peers))

    def gather(kind, s):
        src, dst, dev = (
            ((0, 0), (0, 1), y_peer),
            ((0, 0), (1, 0), z_peer[1]),
            ((0, 0), (2, 0), z_peer[2]),
            ((1, 0), (1, 1), y_peer),
            ((2, 0), (3, 0), z_peer[1]),
            ((2, 0), (2, 1), y_peer),
            ((3, 0), (3, 1), y_peer),
        )[kind]
        return rcopy(
            x_all.at[slot(*src, s)], x_all.at[slot(*dst, s)], ag_send.at[s, kind], ag_recv.at[s, kind], dev
        )

    def c_copy(ch, j):
        rows = rows_of(CHUNKS[ch])
        q = ch * nt + j
        return rcopy(pbuf.at[j, 1 - c, rows], crecv.at[j, rows], c_send.at[q], c_recv.at[q], c_peer)

    def x_copy(part, j):
        rows = rows_of(PARTS[part])
        q = part * nt + j
        return rcopy(xsend.at[j, rows], xrecv.at[j, rows], x_send.at[q], x_recv.at[q], x_peer)

    def h_copy(part, j, h):
        view = hid.at[rows_of(PARTS[part]), side(j, h)]
        q = part * nt + j
        return rcopy(view, view, h_send.at[q], h_recv.at[q], c_peer)

    def up(ch, j):
        rows = rows_of(CHUNKS[ch])
        total = jnp.dot(x_all[rows], w[j], preferred_element_type=f32)
        for h in range(2):
            pbuf[j, h, rows] = total[:, h * half : (h + 1) * half]
        c_copy(ch, j).start()

    def mid(part, j):
        rows = rows_of(PARTS[part])
        total = pbuf[j, c, rows] + crecv[j, rows]
        crecv[j, rows] = total
        xsend[j, rows] = total.astype(bf16)
        x_copy(part, j).start()

    def act(part, j):
        first, last = PARTS[part]
        rows = rows_of(PARTS[part])
        x_copy(part, j).wait_recv()
        bias = bias_u[side(j, c)].astype(f32).reshape(1, half)
        pre = jnp.maximum(crecv[j, rows] + xrecv[j, rows].astype(f32) + bias, 0.0)
        blocks = active.shape[2] // nt
        width = TILE // blocks
        for b in range(blocks // 2):
            lanes = pl.ds(pl.multiple_of(j * TILE + c * half + b * width, width), width)
            gates = [active[s, 0, j * blocks + c * (blocks // 2) + b].astype(f32) for s in range(steps)]
            i = first
            while i < last:
                n = i
                while n < last and ORDER[n][2] == ORDER[i][2]:
                    n += 1
                piece = pre[(i - first) * share : (n - first) * share, b * width : (b + 1) * width]
                hid[pl.ds(i * share, (n - i) * share), lanes] = (piece * gates[ORDER[i][2]]).astype(bf16)
                i = n
        h_copy(part, j, c).start()

    def hidden_ready(part, start, stop):
        @pl.loop(start, stop)
        def _(j):
            h_copy(part, j, 1 - c).wait_recv()

    slots_of = [[i for key in PAIRS[g] for i in (SLOT[key[0], 0, key[1]], SLOT[key[0], 1, key[1]])] for g in range(2)]
    lines_of = [sorted(slots, key=lambda i: i or len(ORDER)) for slots in slots_of]

    def hidden_rows(g, part):
        span = slice(part * depth, (part + 1) * depth)
        ids = lines_of[g]
        if ids[-1] != 0:
            return hid[ids[0] * share : (ids[-1] + 1) * share, span]
        return jnp.concatenate([hid[ids[0] * share : (ids[-2] + 1) * share, span], hid[:share, span]], axis=0)

    def y_copy(g, n):
        q = g * nc + n
        return rcopy(ysend[g].at[n], yrecv[g].at[n], y_send.at[q], y_recv.at[q], y_peer)

    def z_copy(g, n, hop):
        k, first, last = HOPS[g][hop]
        span = pl.ds(first, last - first)
        q = (g * nc + n) * 3 + hop
        return rcopy(zsend[g].at[n, span], zrecv[g].at[n, span], z_send.at[q], z_recv.at[q], z_peer[k])

    def share_out(g, n, total):
        for p, (k, s) in enumerate(PAIRS[g]):
            for e in range(2):
                i = lines_of[g].index(SLOT[k, e, s]) * share
                if e:
                    ysend[g][n, p] = total[i : i + share].astype(bf16)
                else:
                    acc[slot(k, 0, s), cols(n)] = total[i : i + share]
        y_copy(g, n).start()

    def down(n):
        total = jnp.zeros((len(lines_of[0]) * share, TILE), f32)
        for part in range(2):
            total += jnp.dot(hidden_rows(0, part), w[n * 2 + part], preferred_element_type=f32)
        share_out(0, n, total)

    def down_first(n):
        total = jnp.dot(hidden_rows(1, 0), w[n * 2], preferred_element_type=f32)
        for i, line in enumerate(lines_of[1]):
            acc[pl.ds(line * share, share), cols(n)] = total[i * share : (i + 1) * share]

    def down_second(n):
        total = jnp.concatenate([acc[pl.ds(line * share, share), cols(n)] for line in lines_of[1]], axis=0)
        total += jnp.dot(hidden_rows(1, 1), w[n * 2 + 1], preferred_element_type=f32)
        share_out(1, n, total)

    def rs_z(g, n):
        y_copy(g, n).wait_recv()
        for p, (k, s) in enumerate(PAIRS[g]):
            if k:
                pair = acc[slot(k, 0, s), cols(n)] + yrecv[g][n, p].astype(f32)
                zsend[g][n, p - 1] = pair.astype(bf16)
        for hop in range(len(HOPS[g])):
            z_copy(g, n, hop).start()

    def collect(n, g, s):
        total = acc[slot(0, 0, s), cols(n)]
        for p, (k, step) in enumerate(PAIRS[g]):
            if step == s:
                total += (zrecv[g][n, p - 1] if k else yrecv[g][n, p]).astype(f32)
        return total

    def rs_finish(g, n):
        for hop in range(len(HOPS[g])):
            z_copy(g, n, hop).wait_recv()
        if g == 0:
            acc[slot(0, 0, 1), cols(n)] = collect(n, 0, 1)
        total = collect(n, g, g) + bias_d[cols(n)].astype(f32).reshape(1, TILE)
        out[g, :, cols(n)] = total.astype(bf16)
        y_copy(g, n).wait_send()
        for hop in range(len(HOPS[g])):
            z_copy(g, n, hop).wait_send()

    def sent(j, chunks, parts):
        for ch in chunks:
            c_copy(ch, j).wait_send()
        for part in parts:
            x_copy(part, j).wait_send()
            h_copy(part, j, c).wait_send()

    for copy in mine:
        copy.wait()
    for s in (0, 1):
        gather(0, s).start()
        gather(1, s).start()
    gather(1, 0).wait_recv()
    gather(3, 0).start()
    gather(2, 0).start()
    gather(2, 1).start()
    gather(0, 0).wait_recv()

    def first_chunk(j):
        up_load(j).wait()
        up(0, j)

        @pl.when(j >= LAG)
        def _():
            c_copy(0, j - LAG).wait_recv()
            mid(0, j - LAG)

    def forward_far(s):
        gather(2, s).wait_recv()
        gather(4, s).start()
        gather(5, s).start()

    def forward_last(s):
        gather(4, s).wait_recv()
        gather(6, s).start()

    cut = [0, nt // 4, nt // 2, nt * 3 // 4, nt]
    pl.loop(cut[0], cut[1])(first_chunk)
    gather(1, 1).wait_recv()
    gather(3, 1).start()
    pl.loop(cut[1], cut[2])(first_chunk)
    forward_far(0)
    pl.loop(cut[2], cut[3])(first_chunk)
    forward_far(1)
    pl.loop(cut[3], cut[4])(first_chunk)
    forward_last(0)
    gather(3, 0).wait_recv()
    gather(5, 0).wait_recv()

    @pl.loop(0, LAG)
    def _(j):
        up(1, j)
        c_copy(0, nt - LAG + j).wait_recv()
        mid(0, nt - LAG + j)

    forward_last(1)

    @pl.loop(LAG, nt)
    def _(j):
        up(1, j)
        c_copy(1, j - LAG).wait_recv()
        mid(1, j - LAG)
        act(0, j - LAG)

    gather(6, 0).wait_recv()
    for kind in (0, 3, 5, 6):
        gather(kind, 1).wait_recv()

    @pl.loop(0, LAG)
    def _(j):
        up(2, j)
        down_load(j).start()
        c_copy(1, nt - LAG + j).wait_recv()
        mid(1, nt - LAG + j)
        act(0, nt - LAG + j)

    @pl.loop(LAG, nt)
    def _(j):
        up(2, j)
        down_load(j).start()
        c_copy(2, j - LAG).wait_recv()
        mid(2, j - LAG)
        act(1, j - LAG)

    @pl.loop(nt - LAG, nt)
    def _(j):
        c_copy(2, j).wait_recv()
        mid(2, j)
        act(1, j)

    @pl.loop(0, nt)
    def _(j):
        mid(3, j)

    @pl.loop(0, nt)
    def _(j):
        act(2, j)

    for s in range(steps):
        for kind in range(7):
            gather(kind, s).wait_send()

    for part in range(3):
        hidden_ready(part, 0, nt)

    @pl.loop(0, nc)
    def _(n):
        down_load(n * 2).wait()
        down_load(n * 2 + 1).wait()
        down(n)
        act(3, n)
        for i in range(2):
            sent(n * 2 + i, (0, 1), (0, 1))

        @pl.when(n >= LAG)
        def _():
            rs_z(0, n - LAG)

    hidden_ready(3, 0, nc)

    @pl.loop(0, nc)
    def _(n):
        down_first(n)
        act(3, nc + n)
        for i in range(2):
            sent(n * 2 + i, (2,), (2,))

        @pl.when(n >= nc - LAG + 1)
        def _():
            rs_z(0, n - 1)

    hidden_ready(3, nc, nt)

    @pl.loop(0, nc)
    def _(n):
        down_second(n)
        for i in range(2):
            sent(n * 2 + i, (), (3,))

        @pl.when(n == 0)
        def _():
            rs_z(0, nc - 1)

        @pl.when(n >= LAG)
        def _():
            rs_z(1, n - LAG)

    @pl.loop(nc - LAG, nc)
    def _(n):
        rs_z(1, n)

    for g in range(2):
        pl.loop(0, nc)(functools.partial(rs_finish, g))


def fused(groups, tokens, up_weight, up_bias, down_weight, down_bias, active):
    steps, share, depth = tokens.shape
    hidden = up_weight.shape[1]
    nt, nc, rows = hidden // TILE, depth // TILE, steps * groups * share
    f32, bf16 = jnp.float32, jnp.bfloat16
    any_space, vmem = pl.BlockSpec(memory_space=pl.ANY), pl.BlockSpec(memory_space=pltpu.VMEM)
    smem = pl.BlockSpec(memory_space=pltpu.SMEM)
    dma = pltpu.SemaphoreType.DMA
    half = TILE // 2
    return pl.pallas_call(
        functools.partial(fused_kernel, nt),
        out_shape=jax.ShapeDtypeStruct(tokens.shape, bf16),
        in_specs=[any_space, any_space, any_space, vmem, vmem, smem],
        out_specs=vmem,
        scratch_shapes=[
            pltpu.VMEM((rows, depth), bf16),
            pltpu.VMEM((nt, depth, TILE), bf16),
            pltpu.VMEM((nt, 2, rows, half), f32),
            pltpu.VMEM((nt, rows, half), f32),
            pltpu.VMEM((nt, rows, half), bf16),
            pltpu.VMEM((nt, rows, half), bf16),
            pltpu.VMEM((rows, hidden), bf16),
            pltpu.VMEM((rows, depth), f32),
        ]
        + [pltpu.VMEM((nc, len(PAIRS[g]), share, TILE), bf16) for g in (0, 0, 1, 1)]
        + [pltpu.VMEM((nc, len(PAIRS[g]) - 1, share, TILE), bf16) for g in (0, 0, 1, 1)]
        + [
            dma((steps,)),
            dma((nt,)),
            dma((steps, 7)),
            dma((steps, 7)),
        ]
        + [dma((len(CHUNKS) * nt,))] * 2
        + [dma((len(PARTS) * nt,))] * 4
        + [dma((2 * nc,))] * 2
        + [dma((2 * nc * 3,))] * 2,
        compiler_params=pltpu.CompilerParams(
            collective_id=0, has_side_effects=True, vmem_limit_bytes=67043328
        ),
    )(tokens, up_weight, down_weight, up_bias, down_bias, active)


def solution(mesh):
    placed = (
        P(None, "dp", "tensor"),
        P("tensor", "dp"),
        P("dp"),
        P("dp", "tensor"),
        P("tensor"),
        P(None, None, "dp"),
    )
    groups, columns = mesh.shape["dp"], mesh.shape["tensor"]

    def body(*args):
        steps, share, depth = args[0].shape
        hidden, table = args[1].shape[1], args[5].shape
        if (
            (groups, columns, steps, table[1]) == (8, 4, 2, 1)
            and share % 16 == 0
            and depth % TILE == 0
            and hidden == 2 * depth
            and table[2] % (hidden // TILE * 2) == 0
            and depth // TILE > LAG
        ):
            return fused(groups, *args)
        return local(*args)

    return jax.shard_map(
        body, mesh=mesh, in_specs=placed, out_specs=P(None, "dp", "tensor"), check_vma=False
    )
```
